32 devices in a mesh: dp: 8 (over z, y), tensor: 4 (over x, core).
Axes of the slice: x: 2, y: 2, z: 4, core: 2. Of those that a mesh axis runs over, the one named last changes fastest.
Arguments:
- tokens: bfloat16 [2048, 2048], P('dp'), may hold values from -6 to 6
- documents: int32 [8, 256], P('dp'), may hold values from 0 to 7, never falling along the last dimension, each value on 1 to 128 neighbouring positions
- cotangent: bfloat16 [2048, 2048], P('dp'), may hold values from -6 to 6
- qkv_weight: float32 [3, 2048, 2048], P(None, 'dp', 'tensor'), may hold values from -0.1875 to 0.1875
- out_weight: float32 [2048, 2048], P(('tensor', 'dp')), may hold values from -0.25 to 0.25
- lift_weight: float32 [2, 2048, 8192], P(None, 'dp', 'tensor'), may hold values from -0.125 to 0.125
- down_weight: float32 [8192, 2048], P(('tensor', 'dp')), may hold values from -0.0625 to 0.0625
- gains: float32 [2, 2048], P(None, 'dp'), may hold values from 0.5 to 1.5
- qkv_first: float32 [3, 2048, 2048], P(None, 'dp', 'tensor'), may hold values from -3.5 to 3.5
- out_first: float32 [2048, 2048], P(('tensor', 'dp')), may hold values from -3.5 to 3.5
- lift_first: float32 [2, 2048, 8192], P(None, 'dp', 'tensor'), may hold values from -3.5 to 3.5
- down_first: float32 [8192, 2048], P(('tensor', 'dp')), may hold values from -3.5 to 3.5
- gains_first: float32 [2, 2048], P(None, 'dp'), may hold values from -3.5 to 3.5
- qkv_second: float32 [3, 2048, 2048], P(None, 'dp', 'tensor'), may hold values from 0.21038716 to 0.8415486
- out_second: float32 [2048, 2048], P(('tensor', 'dp')), may hold values from 0.21038716 to 0.8415486
- lift_second: float32 [2, 2048, 8192], P(None, 'dp', 'tensor'), may hold values from 0.21038716 to 0.8415486
- down_second: float32 [8192, 2048], P(('tensor', 'dp')), may hold values from 0.21038716 to 0.8415486
- gains_second: float32 [2, 2048], P(None, 'dp'), may hold values from 0.21038716 to 0.8415486
Outputs:
- layer_out: bfloat16 [2048, 2048], P('dp')
- grad_tokens: float32 [2048, 2048], P('dp')
- qkv_new: float32 [3, 2048, 2048], P(None, 'dp', 'tensor')
- out_new: float32 [2048, 2048], P(('tensor', 'dp'))
- lift_new: float32 [2, 2048, 8192], P(None, 'dp', 'tensor')
- down_new: float32 [8192, 2048], P(('tensor', 'dp'))
- gains_new: float32 [2, 2048], P(None, 'dp')
- qkv_moment: float32 [3, 2048, 2048], P(None, 'dp', 'tensor')
- out_moment: float32 [2048, 2048], P(('tensor', 'dp'))
- lift_moment: float32 [2, 2048, 8192], P(None, 'dp', 'tensor')
- down_moment: float32 [8192, 2048], P(('tensor', 'dp'))
- gains_moment: float32 [2, 2048], P(None, 'dp')
- qkv_variance: float32 [3, 2048, 2048], P(None, 'dp', 'tensor')
- out_variance: float32 [2048, 2048], P(('tensor', 'dp'))
- lift_variance: float32 [2, 2048, 8192], P(None, 'dp', 'tensor')
- down_variance: float32 [8192, 2048], P(('tensor', 'dp'))
- gains_variance: float32 [2, 2048], P(None, 'dp')
- grad_norm: float32 [], replicated
The draws below stay inside these ranges and needn't reach their ends.
Inputs may be any that keep to these rules, and one draw needn't show every extreme that they name: Each row of documents is one sequence: ids never fall along the row, and each id is one document of 1 to 128 tokens.
All inputs are finite; a program needn't handle non-finite values.
Results may differ from the reference program's by a relative error of at most 0.015.
The reference program's roundings to bfloat16 on the way count: a program that leaves them out, or rounds other values in their place, can miss the bound.
Values may be sent and summed in bfloat16 or wider, within the bound.
No kernel may reach another device: no remote copies, remote signals or barrier semaphores. Data moves between devices by JAX's collectives and lax.ppermute only.
A program may use at most 256 MiB of HBM per device.

```python
import math
import jax
import jax.numpy as jnp
import numpy as np
from jax import lax

D = 2048
FF = 8192
HD = 128
TOK_DEV = 256
DOCS = 8
STEP = 10
SEQS = 8
TOKENS = 2048
CLIP_NORM = 16384


def levels(stream_key, shape, split, low, largest):
    level, own = 1.0, jax.random.fold_in(stream_key, 6)
    for dim, blocks in split:
        steps = jnp.exp(jax.random.uniform(jax.random.fold_in(own, dim), (blocks,), jnp.float32, low / len(split), largest / len(split)))
        level = level * jnp.repeat(steps, shape[dim] // blocks).reshape([-1 if axis == dim else 1 for axis in range(len(shape))])
    return level


def profile(number_of, total, bound, skew):
    loads = [(1 << 20) // math.isqrt(standing ** skew) + 1 for standing in range(2, number_of + 1)]
    rest, holding = total - bound - (number_of - 1), [1] * (number_of - 1)
    while rest > 0:
        candidates = [i for i in range(number_of - 1) if holding[i] < bound]
        whole, remaining = sum([loads[i] for i in candidates]), rest
        for i in candidates:
            addition = min(bound - holding[i], max(1, remaining * loads[i] // whole), rest)
            holding[i] = holding[i] + addition
            rest = rest - addition
    return np.array([bound] + holding)


def uneven_parts(rng, amount, total, reach, skew):
    if amount == 2:
        one = jax.random.randint(rng, (), max(1, total - reach), min(reach, total - 1) + 1)
        return jnp.stack([one, total - one])
    tallies = jnp.asarray(profile(amount, total, reach, skew), jnp.int32)
    pairs = (amount - 1) // 2
    donor, taker = tallies[1:1 + 2 * pairs:2], tallies[2:2 + 2 * pairs:2]
    margin = jnp.minimum(donor - 1, reach - taker)
    moved = jax.random.randint(jax.random.fold_in(rng, 1), (pairs,), 0, 1 << 20) % (margin + 1)
    tallies = tallies.at[1:1 + 2 * pairs:2].set(donor - moved).at[2:2 + 2 * pairs:2].set(taker + moved)
    return tallies[jax.random.permutation(jax.random.fold_in(rng, 2), amount)]


def bell_draw(rng, shape, spread, most, shards=(), kind=jnp.bfloat16):
    entries = spread * jax.random.normal(rng, shape, jnp.float32)
    if shards:
        entries = entries * levels(rng, shape, shards, -0.22, 0.18)
    return jnp.clip(entries, -most, most).astype(kind)


def setup_inputs(seed: int = 0) -> dict:
    seeds = jax.random.split(jax.random.key(seed), 19)
    tokens = bell_draw(seeds[0], (TOKENS, D), 1.0, 6.0, ((0, 8),))
    documents = jax.vmap(lambda own: jnp.searchsorted(jnp.cumsum(uneven_parts(own, DOCS, TOK_DEV, TOK_DEV // 2, 1)), jnp.arange(TOK_DEV), side="right"))(jax.random.split(seeds[1], SEQS)).reshape((SEQS, TOK_DEV)).astype(jnp.int32)
    cotangent = bell_draw(seeds[2], (TOKENS, D), 1.0, 6.0, ((0, 8),))
    qkv_weight = bell_draw(seeds[3], (3, D, D), (D // 2) ** -0.5, 0.1875, ((1, 8), (2, 4)), jnp.float32)
    out_weight = bell_draw(seeds[4], (D, D), (D // 4) ** -0.5, 0.25, ((0, 32),), jnp.float32)
    lift_weight = bell_draw(seeds[5], (2, D, FF), D ** -0.5, 0.125, ((1, 8), (2, 4)), jnp.float32)
    down_weight = bell_draw(seeds[6], (FF, D), FF ** -0.5, 0.0625, ((0, 32),), jnp.float32)
    gains = jnp.clip(1.0 + 0.1 * jax.random.normal(seeds[7], (2, D), jnp.float32), 0.5, 1.5)
    qkv_first = bell_draw(seeds[8], (3, D, D), (0.111 * 8 * D * (4 * D * D + 3 * D * FF + 2 * D) ** -0.5), 3.5, ((1, 8), (2, 4)), jnp.float32)
    out_first = bell_draw(seeds[9], (D, D), (0.111 * 8 * D * (4 * D * D + 3 * D * FF + 2 * D) ** -0.5), 3.5, ((0, 32),), jnp.float32)
    lift_first = bell_draw(seeds[10], (2, D, FF), (0.111 * 8 * D * (4 * D * D + 3 * D * FF + 2 * D) ** -0.5), 3.5, ((1, 8), (2, 4)), jnp.float32)
    down_first = bell_draw(seeds[11], (FF, D), (0.111 * 8 * D * (4 * D * D + 3 * D * FF + 2 * D) ** -0.5), 3.5, ((0, 32),), jnp.float32)
    gains_first = bell_draw(seeds[12], (2, D), (0.111 * 8 * D * (4 * D * D + 3 * D * FF + 2 * D) ** -0.5), 3.5, ((1, 8),), jnp.float32)
    qkv_second = jnp.clip(jnp.exp(math.log(0.8415486) - 1.3862944 * jax.random.uniform(seeds[13], (3, D, D), jnp.float32) ** levels(seeds[13], (3, D, D), ((1, 8), (2, 4)), -0.2, 0.2)), 0.21038716, 0.8415486)
    out_second = jnp.clip(jnp.exp(math.log(0.8415486) - 1.3862944 * jax.random.uniform(seeds[14], (D, D), jnp.float32) ** levels(seeds[14], (D, D), ((0, 32),), -0.2, 0.2)), 0.21038716, 0.8415486)
    lift_second = jnp.clip(jnp.exp(math.log(0.8415486) - 1.3862944 * jax.random.uniform(seeds[15], (2, D, FF), jnp.float32) ** levels(seeds[15], (2, D, FF), ((1, 8), (2, 4)), -0.2, 0.2)), 0.21038716, 0.8415486)
    down_second = jnp.clip(jnp.exp(math.log(0.8415486) - 1.3862944 * jax.random.uniform(seeds[16], (FF, D), jnp.float32) ** levels(seeds[16], (FF, D), ((0, 32),), -0.2, 0.2)), 0.21038716, 0.8415486)
    gains_second = jnp.clip(jnp.exp(math.log(0.8415486) - 1.3862944 * jax.random.uniform(seeds[17], (2, D), jnp.float32) ** levels(seeds[17], (2, D), ((1, 8),), -0.2, 0.2)), 0.21038716, 0.8415486)
    return {"tokens": tokens, "documents": documents, "cotangent": cotangent, "qkv_weight": qkv_weight, "out_weight": out_weight, "lift_weight": lift_weight, "down_weight": down_weight, "gains": gains, "qkv_first": qkv_first, "out_first": out_first, "lift_first": lift_first, "down_first": down_first, "gains_first": gains_first, "qkv_second": qkv_second, "out_second": out_second, "lift_second": lift_second, "down_second": down_second, "gains_second": gains_second}


norm_eps = 1e-05
beta_one = 0.9
beta_two = 0.95
adam_eps = 1e-08
rate_matrix = 0.02
rate_gain = 0.5
decay_matrix = 0.1
highest = lax.Precision.HIGHEST

@jax.custom_vjp
def low(v):
    return lax.optimization_barrier(v.astype(jnp.bfloat16)).astype(jnp.float32)

@jax.custom_vjp
def low_back(v):
    return v

def low_keep(v):
    return (low(v), None)

def low_pass(kept, grad):
    return (grad,)

def back_keep(v):
    return (v, None)

def back_low(kept, grad):
    return (low(grad),)
low.defvjp(low_keep, low_pass)
low_back.defvjp(back_keep, back_low)

def rms_scale(rows, gain):
    inverse = lax.rsqrt(lax.optimization_barrier(jnp.mean(rows * rows, axis=-1, keepdims=True)) + norm_eps)
    return rows * inverse * gain

def sequence_layer(row_tokens, row_docs, qkv_low, out_low, lift_low, down_low, gains_low):
    length = row_tokens.shape[0]
    heads = qkv_low.shape[2] // HD
    block = min(512, length)
    scale = 1.0 / math.sqrt(HD)
    offset = -math.log(TOK_DEV)
    normed_one = low(rms_scale(row_tokens, gains_low[0]))
    project = jnp.einsum('td,cde->cte', normed_one, qkv_low, precision=highest)
    project = low_back(low(project))
    queries = project[0].reshape(length, heads, HD)
    keys = project[1].reshape(length, heads, HD)
    values = project[2].reshape(length, heads, HD)
    key_pos = jnp.arange(length, dtype=jnp.int32)

    def attend(index):
        start = (index * block).astype(jnp.int32)
        query_block = lax.dynamic_slice_in_dim(queries, start, block, 0)
        query_pos = start + jnp.arange(block, dtype=jnp.int32)
        query_docs = lax.dynamic_slice_in_dim(row_docs, start, block, 0)
        allowed = (query_pos[:, None] >= key_pos[None, :]) & (query_docs[:, None] == row_docs[None, :])
        scores = jnp.einsum('qhd,khd->hqk', query_block, keys, precision=highest) * scale + offset
        scores = low_back(scores)
        probs = low(jnp.where(allowed[None], jax.nn.sigmoid(scores), 0.0))
        return jnp.einsum('hqk,khd->qhd', probs, values, precision=highest)
    attended = lax.map(jax.checkpoint(attend), jnp.arange(length // block, dtype=jnp.int32))
    attended = low_back(low(attended.reshape(length, heads * HD)))
    branch = low_back(jnp.dot(attended, out_low, precision=highest))
    middle = row_tokens + branch
    normed_two = low(rms_scale(middle, gains_low[1]))
    gate_up = jnp.einsum('td,cde->cte', normed_two, lift_low, precision=highest)
    gate_up = low_back(gate_up)
    hidden = low(jax.nn.silu(gate_up[0]) * gate_up[1])
    feed = low_back(jnp.dot(hidden, down_low, precision=highest))
    return middle + feed

def adam_step(weight, first, second, grad, factor, rate, decay):
    clipped = grad * factor
    moment = beta_one * first + (1.0 - beta_one) * clipped
    variance = beta_two * second + (1.0 - beta_two) * clipped * clipped
    corr_one = 1.0 - beta_one ** STEP
    corr_two = 1.0 - beta_two ** STEP
    update = moment / corr_one / (jnp.sqrt(variance / corr_two) + adam_eps)
    return (weight - rate * (update + decay * weight), moment, variance)

def reference(tokens, documents, cotangent, qkv_weight, out_weight, lift_weight, down_weight, gains, qkv_first, out_first, lift_first, down_first, gains_first, qkv_second, out_second, lift_second, down_second, gains_second):

    def forward(tokens_f, qkv_w, out_w, lift_w, down_w, gains_w):
        qkv_low = low(qkv_w)
        out_low = low(out_w)
        lift_low = low(lift_w)
        down_low = low(down_w)
        gains_low = low(gains_w)
        rows = tokens_f.reshape(documents.shape[0], documents.shape[1], tokens_f.shape[1])
        layer_fn = jax.checkpoint(sequence_layer)

        def step(carry, pair):
            return (carry, layer_fn(pair[0], pair[1], qkv_low, out_low, lift_low, down_low, gains_low))
        unused, outputs = lax.scan(step, jnp.zeros((), jnp.float32), (rows, documents))
        return outputs.reshape(tokens_f.shape)
    tokens_f = tokens.astype(jnp.float32)
    layer_f, pullback = jax.vjp(forward, tokens_f, qkv_weight, out_weight, lift_weight, down_weight, gains)
    grad_x, grad_qkv, grad_out, grad_lift, grad_down, grad_gains = pullback(cotangent.astype(jnp.float32))
    total = jnp.sum(grad_qkv * grad_qkv) + jnp.sum(grad_out * grad_out) + jnp.sum(grad_lift * grad_lift) + jnp.sum(grad_down * grad_down) + jnp.sum(grad_gains * grad_gains)
    grad_norm = jnp.sqrt(total)
    factor = CLIP_NORM / jnp.maximum(grad_norm, CLIP_NORM)
    qkv_new, qkv_moment, qkv_variance = adam_step(qkv_weight, qkv_first, qkv_second, grad_qkv, factor, rate_matrix, decay_matrix)
    out_new, out_moment, out_variance = adam_step(out_weight, out_first, out_second, grad_out, factor, rate_matrix, decay_matrix)
    lift_new, lift_moment, lift_variance = adam_step(lift_weight, lift_first, lift_second, grad_lift, factor, rate_matrix, decay_matrix)
    down_new, down_moment, down_variance = adam_step(down_weight, down_first, down_second, grad_down, factor, rate_matrix, decay_matrix)
    gains_new, gains_moment, gains_variance = adam_step(gains, gains_first, gains_second, grad_gains, factor, rate_gain, 0.0)
    return (layer_f.astype(jnp.bfloat16), grad_x, qkv_new, out_new, lift_new, down_new, gains_new, qkv_moment, out_moment, lift_moment, down_moment, gains_moment, qkv_variance, out_variance, lift_variance, down_variance, gains_variance, grad_norm)
```

```python
import math

import jax
import jax.numpy as jnp
from jax import lax
from jax.sharding import PartitionSpec as P

HD = 128
STEP = 10
CLIP_NORM = 16384


norm_eps = 1e-05
beta_one = 0.9
beta_two = 0.95
adam_eps = 1e-08
rate_matrix = 0.02
rate_gain = 0.5
decay_matrix = 0.1


def norm_forward(rows, gain):
    inverse = lax.rsqrt(jnp.mean(rows * rows, axis=-1, keepdims=True) + norm_eps)
    scaled = rows * inverse
    return (scaled, inverse, (scaled * gain).astype(jnp.bfloat16))


def norm_backward(incoming, scaled, inverse, gain):
    grad_gain = jnp.sum(incoming * scaled, axis=0)
    weighted = incoming * gain
    grad_rows = inverse * (weighted - scaled * jnp.mean(weighted * scaled, axis=-1, keepdims=True))
    return (grad_gain, grad_rows)


def block_probs(queries, keys, doc_row, start, block, scale, offset):
    length = keys.shape[0]
    query_pos = start + jnp.arange(block, dtype=jnp.int32)
    key_pos = jnp.arange(length, dtype=jnp.int32)
    allowed = (query_pos[:, None] >= key_pos[None, :]) & (doc_row[:, None] == doc_row[None, :])
    scores = (
        jnp.einsum("qhd,khd->hqk", queries, keys, preferred_element_type=jnp.float32) * scale
        + offset
    )
    probs = jnp.where(allowed[None], jax.nn.sigmoid(scores), 0.0)
    return (queries, probs)


def adam_step(weight, first, second, grad, factor, rate, decay):
    clipped = grad * factor
    moment = beta_one * first + (1.0 - beta_one) * clipped
    variance = beta_two * second + (1.0 - beta_two) * clipped * clipped
    corr_one = 1.0 - beta_one**STEP
    corr_two = 1.0 - beta_two**STEP
    update = moment / corr_one / (jnp.sqrt(variance / corr_two) + adam_eps)
    return (weight - rate * (update + decay * weight), moment, variance)


def on_device(
    tokens,
    documents,
    cotangent,
    qkv_weight,
    out_weight,
    lift_weight,
    down_weight,
    gains,
    qkv_first,
    out_first,
    lift_first,
    down_first,
    gains_first,
    qkv_second,
    out_second,
    lift_second,
    down_second,
    gains_second,
):
    bf16 = jnp.bfloat16
    f32 = jnp.float32
    w_qkv, w_out, w_lift, w_down, w_gains = (
        lax.all_gather(qkv_weight.astype(bf16), "dp", axis=1, tiled=True),
        lax.all_gather(out_weight.astype(bf16), "dp", axis=0, tiled=True),
        lax.all_gather(lift_weight.astype(bf16), "dp", axis=1, tiled=True),
        lax.all_gather(down_weight.astype(bf16), "dp", axis=0, tiled=True),
        lax.all_gather(gains.astype(bf16), "dp", axis=1, tiled=True),
    )
    length = tokens.shape[0]
    local_width = w_qkv.shape[2]
    heads = local_width // HD
    block = min(512, length)
    blocks = length // block
    scale = 1.0 / math.sqrt(HD)
    offset = -math.log(length)
    doc_row = documents[0]
    gain_one = w_gains[0].astype(f32)
    gain_two = w_gains[1].astype(f32)
    x_rows = tokens.astype(f32)
    scaled_one, inverse_one, normed_one = norm_forward(x_rows, gain_one)
    project = jnp.einsum("td,cde->cte", normed_one, w_qkv, preferred_element_type=f32).astype(bf16)
    queries = project[0].reshape(length, heads, HD)
    keys = project[1].reshape(length, heads, HD)
    values = project[2].reshape(length, heads, HD)

    def attend(index):
        start = index * block
        query_block, probs = block_probs(queries, keys, doc_row, start, block, scale, offset)
        return jnp.einsum(
            "hqk,khd->qhd", probs.astype(bf16), values, preferred_element_type=f32
        ).astype(bf16)

    attended = lax.map(attend, jnp.arange(blocks, dtype=jnp.int32)).reshape(length, local_width)
    branch = lax.psum(jnp.dot(attended, w_out, preferred_element_type=f32), "tensor")
    middle = x_rows + branch
    scaled_two, inverse_two, normed_two = norm_forward(middle, gain_two)
    gate_up = jnp.einsum("td,cde->cte", normed_two, w_lift, preferred_element_type=f32)
    gate = gate_up[0]
    upward = gate_up[1]
    sigma = jax.nn.sigmoid(gate)
    hidden = (gate * sigma * upward).astype(bf16)
    feed = lax.psum(
        jnp.dot(hidden, w_down, preferred_element_type=f32).astype(jnp.bfloat16), "tensor"
    ).astype(jnp.float32)
    layer_out = (middle + feed).astype(bf16)
    grad_incoming = cotangent.astype(f32)
    grad_down = jnp.einsum("tf,td->fd", hidden, cotangent, preferred_element_type=f32)
    grad_hidden = jnp.einsum("td,fd->tf", cotangent, w_down, preferred_element_type=f32)
    grad_gate = (grad_hidden * upward * sigma * (1.0 + gate * (1.0 - sigma))).astype(bf16)
    grad_up = (grad_hidden * gate * sigma).astype(bf16)
    grad_pair = jnp.stack([grad_gate, grad_up])
    grad_lift = jnp.einsum("td,ctf->cdf", normed_two, grad_pair, preferred_element_type=f32)
    back_two = lax.psum(
        jnp.einsum("ctf,cdf->td", grad_pair, w_lift, preferred_element_type=f32), "tensor"
    )
    grad_gain_two, grad_mid_norm = norm_backward(back_two, scaled_two, inverse_two, gain_two)
    grad_mid = grad_incoming + grad_mid_norm
    grad_branch = grad_mid.astype(bf16)
    grad_out = jnp.einsum("te,td->ed", attended, grad_branch, preferred_element_type=f32)
    grad_attended = jnp.einsum("td,ed->te", grad_branch, w_out, preferred_element_type=f32).astype(
        bf16
    )
    grad_heads = grad_attended.reshape(length, heads, HD)

    def attend_back(carry, index):
        grad_keys, grad_values = carry
        start = index * block
        query_block, probs = block_probs(queries, keys, doc_row, start, block, scale, offset)
        grad_probs = jnp.einsum("qhd,khd->hqk", grad_heads, values, preferred_element_type=f32)
        grad_scores = (grad_probs * probs * (1.0 - probs)).astype(bf16)
        grad_query = (
            jnp.einsum("hqk,khd->qhd", grad_scores, keys, preferred_element_type=f32) * scale
        )
        grad_keys = (
            grad_keys
            + jnp.einsum("hqk,qhd->khd", grad_scores, query_block, preferred_element_type=f32)
            * scale
        )
        grad_values = grad_values + jnp.einsum(
            "hqk,qhd->khd", probs.astype(bf16), grad_heads, preferred_element_type=f32
        )
        return ((grad_keys, grad_values), grad_query)

    zeros_kv = jnp.zeros((length, heads, HD), f32)
    (grad_keys, grad_values), grad_queries = lax.scan(
        attend_back, (zeros_kv, zeros_kv), jnp.arange(blocks, dtype=jnp.int32)
    )
    grad_project = jnp.stack(
        [
            grad_queries.reshape(length, local_width),
            grad_keys.reshape(length, local_width),
            grad_values.reshape(length, local_width),
        ]
    ).astype(bf16)
    grad_qkv = jnp.einsum("td,cte->cde", normed_one, grad_project, preferred_element_type=f32)
    back_one = lax.psum(
        jnp.einsum("cte,cde->td", grad_project, w_qkv, preferred_element_type=f32), "tensor"
    )
    grad_gain_one, grad_x_norm = norm_backward(back_one, scaled_one, inverse_one, gain_one)
    grad_tokens = grad_mid + grad_x_norm
    grad_gains = jnp.stack([grad_gain_one, grad_gain_two])
    red_qkv, red_out, red_lift, red_down, red_gains = (
        lax.psum_scatter(grad_qkv, "dp", scatter_dimension=1, tiled=True),
        lax.psum_scatter(grad_out, "dp", scatter_dimension=0, tiled=True),
        lax.psum_scatter(grad_lift, "dp", scatter_dimension=1, tiled=True),
        lax.psum_scatter(grad_down, "dp", scatter_dimension=0, tiled=True),
        lax.psum_scatter(grad_gains, "dp", scatter_dimension=1, tiled=True),
    )
    local_total = (
        jnp.sum(red_qkv * red_qkv)
        + jnp.sum(red_out * red_out)
        + jnp.sum(red_lift * red_lift)
        + jnp.sum(red_down * red_down)
        + jnp.sum(red_gains * red_gains) / lax.axis_size("tensor")
    )
    total = lax.psum(local_total, ("dp", "tensor"))
    grad_norm = jnp.sqrt(total)
    factor = CLIP_NORM / jnp.maximum(grad_norm, CLIP_NORM)
    qkv_new, qkv_moment, qkv_variance = adam_step(
        qkv_weight, qkv_first, qkv_second, red_qkv, factor, rate_matrix, decay_matrix
    )
    out_new, out_moment, out_variance = adam_step(
        out_weight, out_first, out_second, red_out, factor, rate_matrix, decay_matrix
    )
    lift_new, lift_moment, lift_variance = adam_step(
        lift_weight, lift_first, lift_second, red_lift, factor, rate_matrix, decay_matrix
    )
    down_new, down_moment, down_variance = adam_step(
        down_weight, down_first, down_second, red_down, factor, rate_matrix, decay_matrix
    )
    gains_new, gains_moment, gains_variance = adam_step(
        gains, gains_first, gains_second, red_gains, factor, rate_gain, 0.0
    )
    return (
        layer_out,
        grad_tokens,
        qkv_new,
        out_new,
        lift_new,
        down_new,
        gains_new,
        qkv_moment,
        out_moment,
        lift_moment,
        down_moment,
        gains_moment,
        qkv_variance,
        out_variance,
        lift_variance,
        down_variance,
        gains_variance,
        grad_norm,
    )


def swap_core(v):
    return lax.ppermute(v, "tensor", [(i, i ^ 1) for i in range(lax.axis_size("tensor"))])


def swap_x(v):
    return lax.ppermute(v, "tensor", [(i, i ^ 2) for i in range(lax.axis_size("tensor"))])


def swap_dp(v, mask):
    return lax.ppermute(v, "dp", [(i, i ^ mask) for i in range(lax.axis_size("dp"))])


def shift_z(v, step):
    size = lax.axis_size("dp")
    return lax.ppermute(v, "dp", [(i, (i + 2 * step) % size) for i in range(size)])


def in_order(first, mine, other, axis):
    return jnp.where(
        first,
        jnp.concatenate([mine, other], axis),
        jnp.concatenate([other, mine], axis),
    )


def gather_rows(own):
    ring = [own]
    for _ in range(lax.axis_size("dp") // 2 - 1):
        ring.append(shift_z(ring[-1], 1))
    return jnp.concatenate(ring + [swap_dp(piece, 1) for piece in ring], 0)


def scatter_rows(partial, rows):
    f32 = jnp.float32
    bf16 = jnp.bfloat16
    ring = lax.axis_size("dp") // 2
    slots = partial.reshape(2, ring, rows, partial.shape[-1])
    held = None
    for step in range(ring - 1, -1, -1):
        here = slots[0, step] + swap_dp(slots[1, step].astype(bf16), 1).astype(f32)
        held = here if held is None else here + shift_z(held.astype(bf16), -1).astype(f32)
    held = held.astype(bf16)
    return held.astype(f32) + swap_x(held).astype(f32)


def on_device_wide(
    tokens,
    documents,
    cotangent,
    qkv_weight,
    out_weight,
    lift_weight,
    down_weight,
    gains,
    qkv_first,
    out_first,
    lift_first,
    down_first,
    gains_first,
    qkv_second,
    out_second,
    lift_second,
    down_second,
    gains_second,
):
    bf16 = jnp.bfloat16
    f32 = jnp.float32
    size = lax.axis_size("dp")
    ring = size // 2
    place = lax.axis_index("dp")
    core = lax.axis_index("tensor") % 2
    first = core == 0
    length, width = tokens.shape
    half = length // 2
    block = qkv_weight.shape[1]
    units = lift_weight.shape[2] // size
    scale = 1.0 / math.sqrt(HD)
    offset = -math.log(length)

    def own_half(v):
        return lax.dynamic_slice_in_dim(v, core * half, half, 0)

    def dot(a, b):
        return jnp.dot(a, b, preferred_element_type=f32)

    def dot_t(a, b):
        return lax.dot_general(a, b, (((1,), (1,)), ((), ())), preferred_element_type=f32)

    def t_dot(a, b):
        return lax.dot_general(a, b, (((0,), (0,)), ((), ())), preferred_element_type=f32)

    w_gains = lax.all_gather(gains.astype(bf16), "dp", axis=1, tiled=True)
    all_docs = lax.all_gather(documents, "dp", axis=0, tiled=True)
    gain_one = w_gains[0].astype(f32)
    gain_two = w_gains[1].astype(f32)

    x_rows = own_half(tokens).astype(f32)
    own_cot = own_half(cotangent)
    scaled_one, inverse_one, normed_one = norm_forward(x_rows, gain_one)
    normed_one = gather_rows(normed_one)

    qkv_low = qkv_weight.astype(bf16).reshape(3, 2, block // 2, qkv_weight.shape[2])
    keep = lax.dynamic_index_in_dim(qkv_low, core, 1, keepdims=False)
    give = lax.dynamic_index_in_dim(qkv_low, 1 - core, 1, keepdims=False)
    plane = in_order(first, keep, swap_core(give), 2)
    w_head = jnp.zeros((size, block // 2, 3 * HD), bf16)
    for delta in range(size):
        piece = lax.dynamic_slice_in_dim(plane, (place ^ delta) * HD, HD, 2)
        piece = jnp.concatenate([piece[0], piece[1], piece[2]], 1)
        if delta:
            piece = swap_dp(piece, delta)
        w_head = lax.dynamic_update_slice_in_dim(w_head, piece[None], place ^ delta, 0)
    w_head = w_head.reshape(size, 1, block // 2, 3 * HD)
    w_head = in_order(first, w_head, swap_core(w_head), 1).reshape(width, 3 * HD)

    to_head = [
        (4 * d + 2 * x + c, 4 * ((size // 2) * c + d // 2) + 2 * x + d % 2)
        for d in range(size)
        for x in range(2)
        for c in range(2)
    ]
    w_rows = lax.ppermute(out_weight.astype(bf16), ("dp", "tensor"), to_head)
    w_rows = in_order(first, w_rows, swap_core(w_rows), 0)

    lift_mine = jnp.zeros((width, 2 * units), bf16)
    for delta in range(size):
        piece = lax.dynamic_slice_in_dim(lift_weight, (place ^ delta) * units, units, 2)
        piece = jnp.concatenate([piece[0], piece[1]], 1).astype(bf16)
        if delta:
            piece = swap_dp(piece, delta)
        lift_mine = lax.dynamic_update_slice_in_dim(lift_mine, piece, (place ^ delta) * block, 0)
    lift_other = swap_core(lift_mine)
    w_lift = jnp.concatenate(
        [lift_mine[:, :units], lift_other[:, :units], lift_mine[:, units:], lift_other[:, units:]], 1
    )
    down_mine = down_weight.astype(bf16)
    w_down = jnp.concatenate([down_mine, swap_core(down_mine)], 0)
    all_cot = gather_rows(own_cot)

    def to_sequences(v):
        v = v.reshape(2, ring, half, v.shape[-1])
        keep = lax.dynamic_index_in_dim(v, core, 0, keepdims=False)
        give = lax.dynamic_index_in_dim(v, 1 - core, 0, keepdims=False)
        return in_order(first, keep, swap_core(give), 1)

    def to_halves(v):
        v = v.reshape(ring, 2, half, v.shape[-1])
        keep = lax.dynamic_index_in_dim(v, core, 1, keepdims=False)
        give = lax.dynamic_index_in_dim(v, 1 - core, 1, keepdims=False)
        joined = in_order(first, keep[None], swap_core(give)[None], 0)
        return joined.reshape(2 * ring * half, v.shape[-1])

    project = to_sequences(dot(normed_one, w_head).astype(bf16))
    queries = project[:, :, :HD]
    keys = project[:, :, HD : 2 * HD]
    values = project[:, :, 2 * HD :]
    owners = ((place // 2 - jnp.arange(ring, dtype=jnp.int32)) % ring) * 2 + (place % 2 ^ core)
    docs = all_docs[owners]
    pos = jnp.arange(length, dtype=jnp.int32)
    allowed = (pos[:, None] >= pos[None, :])[None] & (docs[:, :, None] == docs[:, None, :])
    scores = jnp.einsum("sqd,skd->sqk", queries, keys, preferred_element_type=f32) * scale + offset
    probs = jnp.where(allowed, jax.nn.sigmoid(scores), 0.0)
    probs_low = probs.astype(bf16)
    attended = jnp.einsum("sqk,skd->sqd", probs_low, values, preferred_element_type=f32)
    attended = to_halves(attended.astype(bf16))
    middle = x_rows + scatter_rows(dot(attended, w_rows), half)
    scaled_two, inverse_two, normed_two = norm_forward(middle, gain_two)
    normed_two = gather_rows(normed_two)

    gate_up = dot(normed_two, w_lift)
    gate = gate_up[:, : 2 * units]
    upward = gate_up[:, 2 * units :]
    sigma = jax.nn.sigmoid(gate)
    hidden = (gate * sigma * upward).astype(bf16)
    grad_hidden = dot_t(all_cot, w_down)
    grad_gate = (grad_hidden * upward * sigma * (1.0 + gate * (1.0 - sigma))).astype(bf16)
    grad_up = (grad_hidden * gate * sigma).astype(bf16)
    grad_pair = jnp.concatenate([grad_gate, grad_up], 1)
    back_two = scatter_rows(dot_t(grad_pair, w_lift), half)
    grad_gain_two, grad_mid_norm = norm_backward(back_two, scaled_two, inverse_two, gain_two)
    grad_mid = own_cot.astype(f32) + grad_mid_norm
    all_branch = gather_rows(grad_mid.astype(bf16))

    feed = scatter_rows(dot(hidden, w_down), half)
    layer_half = (middle + feed).astype(bf16)
    layer_out = in_order(first, layer_half, swap_core(layer_half), 0)

    grad_down = t_dot(hidden, all_cot)
    red_down = grad_down[:block] + swap_core(grad_down[block:])
    lift_give = t_dot(
        normed_two, jnp.concatenate([grad_gate[:, units:], grad_up[:, units:]], 1)
    )
    lift_keep = t_dot(
        normed_two, jnp.concatenate([grad_gate[:, :units], grad_up[:, :units]], 1)
    )
    lift_sum = (lift_keep + swap_core(lift_give)).astype(bf16)
    red_lift = jnp.zeros(lift_weight.shape, f32)
    for delta in range(size):
        piece = lax.dynamic_slice_in_dim(lift_sum, (place ^ delta) * block, block, 0)
        if delta:
            piece = swap_dp(piece, delta)
        piece = jnp.stack([piece[:, :units], piece[:, units:]]).astype(f32)
        red_lift = lax.dynamic_update_slice_in_dim(red_lift, piece, (place ^ delta) * units, 2)

    grad_out = t_dot(attended, all_branch)
    rows = HD // 2
    out_keep = lax.dynamic_slice_in_dim(grad_out, core * rows, rows, 0)
    out_give = lax.dynamic_slice_in_dim(grad_out, (1 - core) * rows, rows, 0)
    red_out = (out_keep + swap_core(out_give)).astype(bf16)
    red_out = lax.ppermute(red_out, ("dp", "tensor"), [(b, a) for a, b in to_head]).astype(f32)

    grad_heads = to_sequences(dot_t(all_branch, w_rows).astype(bf16))
    grad_probs = jnp.einsum("sqd,skd->sqk", grad_heads, values, preferred_element_type=f32)
    grad_scores = (grad_probs * probs * (1.0 - probs)).astype(bf16)
    grad_queries = jnp.einsum("sqk,skd->sqd", grad_scores, keys, preferred_element_type=f32) * scale
    grad_keys = jnp.einsum("sqk,sqd->skd", grad_scores, queries, preferred_element_type=f32) * scale
    grad_values = jnp.einsum("sqk,sqd->skd", probs_low, grad_heads, preferred_element_type=f32)
    grad_project = to_halves(
        jnp.concatenate([grad_queries, grad_keys, grad_values], 2).astype(bf16)
    )
    back_one = scatter_rows(dot_t(grad_project, w_head), half)

    grad_head = t_dot(normed_one, grad_project).reshape(size, 2, block // 2, 3 * HD)
    keep = lax.dynamic_index_in_dim(grad_head, core, 1, keepdims=False)
    give = lax.dynamic_index_in_dim(grad_head, 1 - core, 1, keepdims=False)
    grad_head = (keep + swap_core(give)).astype(bf16)
    by_head = jnp.zeros(grad_head.shape, bf16)
    for delta in range(size):
        piece = lax.dynamic_slice_in_dim(grad_head, place ^ delta, 1, 0)
        if delta:
            piece = swap_dp(piece, delta)
        by_head = lax.dynamic_update_slice_in_dim(by_head, piece, place ^ delta, 0)
    keep = lax.dynamic_slice_in_dim(by_head, core * ring, ring, 0)
    give = lax.dynamic_slice_in_dim(by_head, (1 - core) * ring, ring, 0)
    red_qkv = in_order(first, keep, swap_core(give), 1)
    red_qkv = red_qkv.reshape(ring, block, 3, HD).transpose(2, 1, 0, 3)
    red_qkv = red_qkv.reshape(qkv_weight.shape).astype(f32)

    grad_gain_one, grad_x_norm = norm_backward(back_one, scaled_one, inverse_one, gain_one)
    tokens_half = grad_mid + grad_x_norm
    grad_tokens = in_order(first, tokens_half, swap_core(tokens_half), 0)

    grad_gains = 0.5 * jnp.stack([grad_gain_one, grad_gain_two])
    local_total = (
        jnp.sum(red_qkv * red_qkv)
        + jnp.sum(red_out * red_out)
        + jnp.sum(red_lift * red_lift)
        + jnp.sum(red_down * red_down)
    )
    grad_gains, total = lax.psum((grad_gains, local_total), ("dp", "tensor"))
    grad_norm = jnp.sqrt(total + jnp.sum(grad_gains * grad_gains))
    red_gains = lax.dynamic_slice_in_dim(grad_gains, place * gains.shape[1], gains.shape[1], 1)
    factor = CLIP_NORM / jnp.maximum(grad_norm, CLIP_NORM)
    qkv_new, qkv_moment, qkv_variance = adam_step(
        qkv_weight, qkv_first, qkv_second, red_qkv, factor, rate_matrix, decay_matrix
    )
    out_new, out_moment, out_variance = adam_step(
        out_weight, out_first, out_second, red_out, factor, rate_matrix, decay_matrix
    )
    lift_new, lift_moment, lift_variance = adam_step(
        lift_weight, lift_first, lift_second, red_lift, factor, rate_matrix, decay_matrix
    )
    down_new, down_moment, down_variance = adam_step(
        down_weight, down_first, down_second, red_down, factor, rate_matrix, decay_matrix
    )
    gains_new, gains_moment, gains_variance = adam_step(
        gains, gains_first, gains_second, red_gains, factor, rate_gain, 0.0
    )
    return (
        layer_out,
        grad_tokens,
        qkv_new,
        out_new,
        lift_new,
        down_new,
        gains_new,
        qkv_moment,
        out_moment,
        lift_moment,
        down_moment,
        gains_moment,
        qkv_variance,
        out_variance,
        lift_variance,
        down_variance,
        gains_variance,
        grad_norm,
    )


def solution(mesh):
    placed = (
        P("dp", None),
        P("dp", None),
        P("dp", None),
        P(None, "dp", "tensor"),
        P(("tensor", "dp"), None),
        P(None, "dp", "tensor"),
        P(("tensor", "dp"), None),
        P(None, "dp"),
        P(None, "dp", "tensor"),
        P(("tensor", "dp"), None),
        P(None, "dp", "tensor"),
        P(("tensor", "dp"), None),
        P(None, "dp"),
        P(None, "dp", "tensor"),
        P(("tensor", "dp"), None),
        P(None, "dp", "tensor"),
        P(("tensor", "dp"), None),
        P(None, "dp"),
    )
    def layer(*arrays):
        plane_heads = 2 * arrays[3].shape[2] // HD
        wide = lax.axis_size("tensor") == 4 and lax.axis_size("dp") == plane_heads
        return (on_device_wide if wide else on_device)(*arrays)

    return jax.shard_map(
        layer,
        mesh=mesh,
        in_specs=placed,
        out_specs=(
            P("dp", None),
            P("dp", None),
            P(None, "dp", "tensor"),
            P(("tensor", "dp"), None),
            P(None, "dp", "tensor"),
            P(("tensor", "dp"), None),
            P(None, "dp"),
            P(None, "dp", "tensor"),
            P(("tensor", "dp"), None),
            P(None, "dp", "tensor"),
            P(("tensor", "dp"), None),
            P(None, "dp"),
            P(None, "dp", "tensor"),
            P(("tensor", "dp"), None),
            P(None, "dp", "tensor"),
            P(("tensor", "dp"), None),
            P(None, "dp"),
            P(),
        ),
        check_vma=False,
    )
```

```python
import math

import jax
import jax.numpy as jnp
from jax import lax
from jax.sharding import PartitionSpec as P

HD = 128
STEP = 10
CLIP_NORM = 16384


norm_eps = 1e-05
beta_one = 0.9
beta_two = 0.95
adam_eps = 1e-08
rate_matrix = 0.02
rate_gain = 0.5
decay_matrix = 0.1


def norm_forward(rows, gain):
    inverse = lax.rsqrt(jnp.mean(rows * rows, axis=-1, keepdims=True) + norm_eps)
    scaled = rows * inverse
    return (scaled, inverse, (scaled * gain).astype(jnp.bfloat16))


def norm_backward(incoming, scaled, inverse, gain):
    grad_gain = jnp.sum(incoming * scaled, axis=0)
    weighted = incoming * gain
    grad_rows = inverse * (weighted - scaled * jnp.mean(weighted * scaled, axis=-1, keepdims=True))
    return (grad_gain, grad_rows)


def block_probs(queries, keys, doc_row, start, block, scale, offset):
    length = keys.shape[0]
    query_pos = start + jnp.arange(block, dtype=jnp.int32)
    key_pos = jnp.arange(length, dtype=jnp.int32)
    allowed = (query_pos[:, None] >= key_pos[None, :]) & (doc_row[:, None] == doc_row[None, :])
    scores = (
        jnp.einsum("qhd,khd->hqk", queries, keys, preferred_element_type=jnp.float32) * scale
        + offset
    )
    probs = jnp.where(allowed[None], jax.nn.sigmoid(scores), 0.0)
    return (queries, probs)


def adam_step(weight, first, second, grad, factor, rate, decay):
    clipped = grad * factor
    moment = beta_one * first + (1.0 - beta_one) * clipped
    variance = beta_two * second + (1.0 - beta_two) * clipped * clipped
    corr_one = 1.0 - beta_one**STEP
    corr_two = 1.0 - beta_two**STEP
    update = moment / corr_one / (jnp.sqrt(variance / corr_two) + adam_eps)
    return (weight - rate * (update + decay * weight), moment, variance)


def on_device(
    tokens,
    documents,
    cotangent,
    qkv_weight,
    out_weight,
    lift_weight,
    down_weight,
    gains,
    qkv_first,
    out_first,
    lift_first,
    down_first,
    gains_first,
    qkv_second,
    out_second,
    lift_second,
    down_second,
    gains_second,
):
    bf16 = jnp.bfloat16
    f32 = jnp.float32
    w_qkv, w_out, w_lift, w_down, w_gains = (
        lax.all_gather(qkv_weight.astype(bf16), "dp", axis=1, tiled=True),
        lax.all_gather(out_weight.astype(bf16), "dp", axis=0, tiled=True),
        lax.all_gather(lift_weight.astype(bf16), "dp", axis=1, tiled=True),
        lax.all_gather(down_weight.astype(bf16), "dp", axis=0, tiled=True),
        lax.all_gather(gains.astype(bf16), "dp", axis=1, tiled=True),
    )
    length = tokens.shape[0]
    local_width = w_qkv.shape[2]
    heads = local_width // HD
    block = min(512, length)
    blocks = length // block
    scale = 1.0 / math.sqrt(HD)
    offset = -math.log(length)
    doc_row = documents[0]
    gain_one = w_gains[0].astype(f32)
    gain_two = w_gains[1].astype(f32)
    x_rows = tokens.astype(f32)
    scaled_one, inverse_one, normed_one = norm_forward(x_rows, gain_one)
    project = jnp.einsum("td,cde->cte", normed_one, w_qkv, preferred_element_type=f32).astype(bf16)
    queries = project[0].reshape(length, heads, HD)
    keys = project[1].reshape(length, heads, HD)
    values = project[2].reshape(length, heads, HD)

    def attend(index):
        start = index * block
        query_block, probs = block_probs(queries, keys, doc_row, start, block, scale, offset)
        return jnp.einsum(
            "hqk,khd->qhd", probs.astype(bf16), values, preferred_element_type=f32
        ).astype(bf16)

    attended = lax.map(attend, jnp.arange(blocks, dtype=jnp.int32)).reshape(length, local_width)
    branch = lax.psum(jnp.dot(attended, w_out, preferred_element_type=f32), "tensor")
    middle = x_rows + branch
    scaled_two, inverse_two, normed_two = norm_forward(middle, gain_two)
    gate_up = jnp.einsum("td,cde->cte", normed_two, w_lift, preferred_element_type=f32)
    gate = gate_up[0]
    upward = gate_up[1]
    sigma = jax.nn.sigmoid(gate)
    hidden = (gate * sigma * upward).astype(bf16)
    feed = lax.psum(
        jnp.dot(hidden, w_down, preferred_element_type=f32).astype(jnp.bfloat16), "tensor"
    ).astype(jnp.float32)
    layer_out = (middle + feed).astype(bf16)
    grad_incoming = cotangent.astype(f32)
    grad_down = jnp.einsum("tf,td->fd", hidden, cotangent, preferred_element_type=f32)
    grad_hidden = jnp.einsum("td,fd->tf", cotangent, w_down, preferred_element_type=f32)
    grad_gate = (grad_hidden * upward * sigma * (1.0 + gate * (1.0 - sigma))).astype(bf16)
    grad_up = (grad_hidden * gate * sigma).astype(bf16)
    grad_pair = jnp.stack([grad_gate, grad_up])
    grad_lift = jnp.einsum("td,ctf->cdf", normed_two, grad_pair, preferred_element_type=f32)
    back_two = lax.psum(
        jnp.einsum("ctf,cdf->td", grad_pair, w_lift, preferred_element_type=f32), "tensor"
    )
    grad_gain_two, grad_mid_norm = norm_backward(back_two, scaled_two, inverse_two, gain_two)
    grad_mid = grad_incoming + grad_mid_norm
    grad_branch = grad_mid.astype(bf16)
    grad_out = jnp.einsum("te,td->ed", attended, grad_branch, preferred_element_type=f32)
    grad_attended = jnp.einsum("td,ed->te", grad_branch, w_out, preferred_element_type=f32).astype(
        bf16
    )
    grad_heads = grad_attended.reshape(length, heads, HD)

    def attend_back(carry, index):
        grad_keys, grad_values = carry
        start = index * block
        query_block, probs = block_probs(queries, keys, doc_row, start, block, scale, offset)
        grad_probs = jnp.einsum("qhd,khd->hqk", grad_heads, values, preferred_element_type=f32)
        grad_scores = (grad_probs * probs * (1.0 - probs)).astype(bf16)
        grad_query = (
            jnp.einsum("hqk,khd->qhd", grad_scores, keys, preferred_element_type=f32) * scale
        )
        grad_keys = (
            grad_keys
            + jnp.einsum("hqk,qhd->khd", grad_scores, query_block, preferred_element_type=f32)
            * scale
        )
        grad_values = grad_values + jnp.einsum(
            "hqk,qhd->khd", probs.astype(bf16), grad_heads, preferred_element_type=f32
        )
        return ((grad_keys, grad_values), grad_query)

    zeros_kv = jnp.zeros((length, heads, HD), f32)
    (grad_keys, grad_values), grad_queries = lax.scan(
        attend_back, (zeros_kv, zeros_kv), jnp.arange(blocks, dtype=jnp.int32)
    )
    grad_project = jnp.stack(
        [
            grad_queries.reshape(length, local_width),
            grad_keys.reshape(length, local_width),
            grad_values.reshape(length, local_width),
        ]
    ).astype(bf16)
    grad_qkv = jnp.einsum("td,cte->cde", normed_one, grad_project, preferred_element_type=f32)
    back_one = lax.psum(
        jnp.einsum("cte,cde->td", grad_project, w_qkv, preferred_element_type=f32), "tensor"
    )
    grad_gain_one, grad_x_norm = norm_backward(back_one, scaled_one, inverse_one, gain_one)
    grad_tokens = grad_mid + grad_x_norm
    grad_gains = jnp.stack([grad_gain_one, grad_gain_two])
    red_qkv, red_out, red_lift, red_down, red_gains = (
        lax.psum_scatter(grad_qkv, "dp", scatter_dimension=1, tiled=True),
        lax.psum_scatter(grad_out, "dp", scatter_dimension=0, tiled=True),
        lax.psum_scatter(grad_lift, "dp", scatter_dimension=1, tiled=True),
        lax.psum_scatter(grad_down, "dp", scatter_dimension=0, tiled=True),
        lax.psum_scatter(grad_gains, "dp", scatter_dimension=1, tiled=True),
    )
    local_total = (
        jnp.sum(red_qkv * red_qkv)
        + jnp.sum(red_out * red_out)
        + jnp.sum(red_lift * red_lift)
        + jnp.sum(red_down * red_down)
        + jnp.sum(red_gains * red_gains) / lax.axis_size("tensor")
    )
    total = lax.psum(local_total, ("dp", "tensor"))
    grad_norm = jnp.sqrt(total)
    factor = CLIP_NORM / jnp.maximum(grad_norm, CLIP_NORM)
    qkv_new, qkv_moment, qkv_variance = adam_step(
        qkv_weight, qkv_first, qkv_second, red_qkv, factor, rate_matrix, decay_matrix
    )
    out_new, out_moment, out_variance = adam_step(
        out_weight, out_first, out_second, red_out, factor, rate_matrix, decay_matrix
    )
    lift_new, lift_moment, lift_variance = adam_step(
        lift_weight, lift_first, lift_second, red_lift, factor, rate_matrix, decay_matrix
    )
    down_new, down_moment, down_variance = adam_step(
        down_weight, down_first, down_second, red_down, factor, rate_matrix, decay_matrix
    )
    gains_new, gains_moment, gains_variance = adam_step(
        gains, gains_first, gains_second, red_gains, factor, rate_gain, 0.0
    )
    return (
        layer_out,
        grad_tokens,
        qkv_new,
        out_new,
        lift_new,
        down_new,
        gains_new,
        qkv_moment,
        out_moment,
        lift_moment,
        down_moment,
        gains_moment,
        qkv_variance,
        out_variance,
        lift_variance,
        down_variance,
        gains_variance,
        grad_norm,
    )


def swap_tensor(v, mask):
    return lax.ppermute(v, "tensor", [(i, i ^ mask) for i in range(lax.axis_size("tensor"))])


def swap_dp(v, mask):
    return lax.ppermute(v, "dp", [(i, i ^ mask) for i in range(lax.axis_size("dp"))])


def shift_z(v, step):
    size = lax.axis_size("dp")
    return lax.ppermute(v, "dp", [(i, (i + 2 * step) % size) for i in range(size)])


def put(buffer, piece, index, axis):
    return lax.dynamic_update_slice_in_dim(buffer, piece, index, axis)


def after(v, *earlier):
    return lax.optimization_barrier((v, earlier))[0]


def across(v):
    return lax.all_to_all(v, "dp", 0, 0, tiled=True)


def exchange(pieces, swap, place, like, axis):
    buffer = None
    for delta in range(lax.axis_size("dp") if swap is swap_dp else lax.axis_size("tensor")):
        piece = pieces(place ^ delta)
        if delta:
            piece = swap(piece, delta)
        if buffer is None:
            buffer = jnp.zeros(like, piece.dtype)
        buffer = put(buffer, piece, (place ^ delta) * piece.shape[axis], axis)
    return buffer


def four(mine):
    far = swap_tensor(mine, 2)
    return [mine, swap_tensor(mine, 1), far, swap_tensor(far, 1)]


def join_four(mine, place, axis):
    shape = list(mine.shape)
    shape[axis] *= 4
    buffer = jnp.zeros(shape, mine.dtype)
    for delta, piece in enumerate(four(mine)):
        buffer = put(buffer, piece, (place ^ delta) * mine.shape[axis], axis)
    return buffer


def reduce_far(piece_of):
    far = swap_tensor(piece_of(3).astype(jnp.bfloat16), 1).astype(jnp.float32) + piece_of(2)
    return far.astype(jnp.bfloat16)


def reduce_four(far, piece_of):
    near = swap_tensor(piece_of(1).astype(jnp.bfloat16), 1).astype(jnp.float32) + piece_of(0)
    return near + swap_tensor(far, 2).astype(jnp.float32)


def gather_rows(own):
    ring = lax.axis_size("dp") // 2
    moved = {step: shift_z(own, step) for step in (1, ring - 1, *range(2, ring - 1))}
    column = [own] + [moved[step] for step in range(1, ring)]
    other = [swap_dp(piece, 1) for piece in column]
    return jnp.concatenate(column + other, 0)


def scatter_rows(partial, rows):
    f32 = jnp.float32
    bf16 = jnp.bfloat16
    ring = lax.axis_size("dp") // 2
    slots = partial.reshape(2, ring, rows, partial.shape[-1])
    here = {
        step: slots[0, step] + swap_dp(slots[1, step].astype(bf16), 1).astype(f32)
        for step in (*range(ring - 2, 0, -1), ring - 1, 0)
    }
    total = here[0]
    for step in (*range(ring - 2, 0, -1), ring - 1):
        total = total + shift_z(here[step].astype(bf16), -step).astype(f32)
    return total


def on_device_wide(
    tokens,
    documents,
    cotangent,
    qkv_weight,
    out_weight,
    lift_weight,
    down_weight,
    gains,
    qkv_first,
    out_first,
    lift_first,
    down_first,
    gains_first,
    qkv_second,
    out_second,
    lift_second,
    down_second,
    gains_second,
):
    bf16 = jnp.bfloat16
    f32 = jnp.float32
    size = lax.axis_size("dp")
    ring = size // 2
    place = lax.axis_index("dp")
    part = lax.axis_index("tensor")
    length, width = tokens.shape
    rows = length // 4
    block = qkv_weight.shape[1]
    quarter = block // 4
    units = lift_weight.shape[2] // size
    pair = 2 * HD
    scale = 1.0 / math.sqrt(HD)
    offset = -math.log(length)

    def own_rows(v):
        return lax.dynamic_slice_in_dim(v, part * rows, rows, 0)

    def take(v, index, axis):
        return lax.dynamic_index_in_dim(v, index, axis, keepdims=True)

    def dot(a, b):
        return jnp.dot(a, b, preferred_element_type=f32)

    def dot_t(a, b):
        return lax.dot_general(a, b, (((1,), (1,)), ((), ())), preferred_element_type=f32)

    def t_dot(a, b):
        return lax.dot_general(a, b, (((0,), (0,)), ((), ())), preferred_element_type=f32)

    small = jnp.concatenate([gains, documents.astype(f32)], 0)[None]
    small = exchange(lambda k: small, swap_dp, place, (size,) + small.shape[1:], 0)
    w_gains = small[:, :2].transpose(1, 0, 2).reshape(2, width).astype(bf16).astype(f32)
    gain_one = w_gains[0]
    gain_two = w_gains[1]

    own_tokens = own_rows(tokens)
    own_cot = own_rows(cotangent)
    all_tokens = gather_rows(own_tokens)
    x_rows = own_tokens.astype(f32)

    qkv_low = qkv_weight.astype(bf16).reshape(3, 4, quarter, qkv_weight.shape[2])
    plane = exchange(
        lambda k: take(qkv_low, k, 1)[:, 0],
        swap_tensor,
        part,
        (3, quarter, 4 * qkv_weight.shape[2]),
        2,
    )

    w_head = plane.reshape(3, quarter, size, pair).transpose(2, 1, 0, 3)
    w_head = across(w_head.reshape(size, quarter, 3 * pair))
    lift_weight_late = after(lift_weight, w_head)
    own_cot = after(own_cot, w_head)
    w_head = join_four(w_head[:, None], part, 1).reshape(width, 3 * pair)

    to_head = [
        (4 * d + t, 4 * (2 * t + d // 4) + d % 4) for d in range(size) for t in range(4)
    ]
    w_rows = lax.ppermute(out_weight.astype(bf16), ("dp", "tensor"), to_head)
    w_rows = join_four(w_rows, part, 0)

    w_down = jnp.concatenate(four(after(down_weight, w_head).astype(bf16)), 0)

    w_lift = lift_weight_late.astype(bf16).reshape(2, block, size, units).transpose(2, 1, 0, 3)
    w_lift = across(w_lift.reshape(size, block, 2 * units))
    w_lift = four(w_lift.reshape(width, 2 * units))
    w_lift = jnp.concatenate([v[:, :units] for v in w_lift] + [v[:, units:] for v in w_lift], 1)
    all_cot = gather_rows(own_cot)

    def to_sequences(v):
        v = v.reshape(4, 2, 1, rows, v.shape[-1])
        v = exchange(
            lambda k: take(v, k, 0)[0], swap_tensor, part, (2, 4) + v.shape[3:], 1
        )
        return v.reshape(2, length, v.shape[-1])

    def to_quarters(v):
        v = v.reshape(2, 4, rows, v.shape[-1])
        v = exchange(
            lambda k: take(v, k, 1)[None, :, 0], swap_tensor, part, (4, 2) + v.shape[2:], 0
        )
        return v.reshape(2 * size // 2 * rows, v.shape[-1])

    normed_one = norm_forward(all_tokens.astype(f32), gain_one)[2]
    project = to_sequences(dot(normed_one, w_head).astype(bf16))
    project = project.reshape(2, length, 6, HD)
    queries = project[:, :, 0:2]
    keys = project[:, :, 2:4]
    values = project[:, :, 4:6]
    docs = jnp.concatenate(
        [
            take(
                small[:, 2],
                (place // 2 - 2 * (part % 2) - s) % ring * 2 + (place % 2 ^ part // 2),
                0,
            )
            for s in range(2)
        ],
        0,
    )
    pos = jnp.arange(length, dtype=jnp.int32)
    allowed = (pos[:, None] >= pos[None, :])[None] & (docs[:, :, None] == docs[:, None, :])
    scores = jnp.einsum("sqhd,skhd->shqk", queries, keys, preferred_element_type=f32)
    scores = scores * scale + offset
    probs = jnp.where(allowed[:, None], jax.nn.sigmoid(scores), 0.0)
    probs_low = probs.astype(bf16)
    attended = jnp.einsum("shqk,skhd->sqhd", probs_low, values, preferred_element_type=f32)
    attended = to_quarters(attended.astype(bf16).reshape(2, length, pair))
    middle = x_rows + scatter_rows(dot(attended, w_rows), rows)
    scaled_two, inverse_two, normed_two = norm_forward(middle, gain_two)
    normed_two = gather_rows(normed_two)

    gate_up = dot(normed_two, w_lift)
    gate = gate_up[:, : 4 * units]
    upward = gate_up[:, 4 * units :]
    sigma = jax.nn.sigmoid(gate)
    hidden = (gate * sigma * upward).astype(bf16)
    grad_hidden = dot_t(all_cot, w_down)
    grad_gate = (grad_hidden * upward * sigma * (1.0 + gate * (1.0 - sigma))).astype(bf16)
    grad_up = (grad_hidden * gate * sigma).astype(bf16)
    grad_pair = jnp.concatenate([grad_gate, grad_up], 1)
    back_two = scatter_rows(dot_t(grad_pair, w_lift), rows)

    def unit_block(v, delta):
        return v[:, delta * units : (delta + 1) * units]

    def down_piece(delta):
        return t_dot(unit_block(hidden, delta), all_cot)

    def lift_piece(delta):
        own = [unit_block(grad_gate, delta), unit_block(grad_up, delta)]
        return t_dot(normed_two, jnp.concatenate(own, 1))

    lift_far = reduce_far(lift_piece)
    down_far = reduce_far(down_piece)
    back_two = after(back_two, lift_far, down_far)
    grad_gain_two, grad_mid_norm = norm_backward(back_two, scaled_two, inverse_two, gain_two)
    grad_mid = own_cot.astype(f32) + grad_mid_norm
    all_branch = gather_rows(grad_mid.astype(bf16))

    lift_sum = reduce_four(lift_far, lift_piece).astype(bf16)
    red_down = reduce_four(down_far, down_piece)
    red_lift = across(lift_sum.reshape(size, block, 2 * units)).reshape(size, block, 2, units)
    red_lift = red_lift.transpose(2, 1, 0, 3).reshape(lift_weight.shape).astype(f32)

    grad_out = t_dot(attended, all_branch).reshape(4, pair // 4, width)

    def out_piece(delta):
        return take(grad_out, part ^ delta, 0)[0]

    red_out = reduce_four(reduce_far(out_piece), out_piece).astype(bf16)
    red_out = lax.ppermute(red_out, ("dp", "tensor"), [(b, a) for a, b in to_head]).astype(f32)

    grad_heads = to_sequences(dot_t(all_branch, w_rows).astype(bf16))
    grad_heads = grad_heads.reshape(2, length, 2, HD)
    grad_probs = jnp.einsum("sqhd,skhd->shqk", grad_heads, values, preferred_element_type=f32)
    grad_scores = (grad_probs * probs * (1.0 - probs)).astype(bf16)
    grad_queries = jnp.einsum("shqk,skhd->sqhd", grad_scores, keys, preferred_element_type=f32)
    grad_keys = jnp.einsum("shqk,sqhd->skhd", grad_scores, queries, preferred_element_type=f32)
    grad_values = jnp.einsum("shqk,sqhd->skhd", probs_low, grad_heads, preferred_element_type=f32)
    grad_project = jnp.concatenate([grad_queries * scale, grad_keys * scale, grad_values], 2)
    grad_project = to_quarters(grad_project.astype(bf16).reshape(2, length, 3 * pair))
    grad_project = after(grad_project, lift_sum)
    back_one = scatter_rows(dot_t(grad_project, w_head), rows)

    grad_head = t_dot(normed_one, grad_project).reshape(size, 4, quarter, 3 * pair)

    def head_piece(delta):
        return take(grad_head, part ^ delta, 1)[:, 0]

    grad_head_sum = reduce_four(reduce_far(head_piece), head_piece).astype(bf16)
    by_head = across(grad_head_sum).reshape(4, 2, quarter, 3, pair).transpose(0, 3, 2, 1, 4)
    by_head = by_head.reshape(4, 3, quarter, 2 * pair)
    red_qkv = exchange(
        lambda k: take(by_head, k, 0)[0], swap_tensor, part, qkv_weight.shape, 1
    ).astype(f32)

    scaled_one, inverse_one, unused = norm_forward(x_rows, gain_one)
    grad_gain_one, grad_x_norm = norm_backward(back_one, scaled_one, inverse_one, gain_one)
    grad_tokens = join_four(grad_mid + grad_x_norm, part, 0)

    feed = scatter_rows(dot(after(hidden, back_one), w_down), rows)
    layer_out = join_four((middle + feed).astype(bf16), part, 0)

    local_total = (
        jnp.sum(red_qkv * red_qkv)
        + jnp.sum(red_out * red_out)
        + jnp.sum(red_lift * red_lift)
        + jnp.sum(red_down * red_down)
    )
    totals = jnp.concatenate(
        [
            jnp.stack([grad_gain_one, grad_gain_two]).reshape(-1, 128),
            jnp.broadcast_to(local_total, (8, 128)),
        ]
    )
    for swap, index, members in ((swap_tensor, part, 4), (swap_dp, place, size)):
        sent = totals[None]
        totals = exchange(lambda k: sent, swap, index, (members,) + sent.shape[1:], 0).sum(0)
    grad_gains = totals[:-8].reshape(2, width)
    grad_norm = jnp.sqrt(totals[-1, 0] + jnp.sum(grad_gains * grad_gains))
    red_gains = lax.dynamic_slice_in_dim(grad_gains, place * gains.shape[1], gains.shape[1], 1)
    factor = CLIP_NORM / jnp.maximum(grad_norm, CLIP_NORM)
    qkv_new, qkv_moment, qkv_variance = adam_step(
        qkv_weight, qkv_first, qkv_second, red_qkv, factor, rate_matrix, decay_matrix
    )
    out_new, out_moment, out_variance = adam_step(
        out_weight, out_first, out_second, red_out, factor, rate_matrix, decay_matrix
    )
    lift_new, lift_moment, lift_variance = adam_step(
        lift_weight, lift_first, lift_second, red_lift, factor, rate_matrix, decay_matrix
    )
    down_new, down_moment, down_variance = adam_step(
        down_weight, down_first, down_second, red_down, factor, rate_matrix, decay_matrix
    )
    gains_new, gains_moment, gains_variance = adam_step(
        gains, gains_first, gains_second, red_gains, factor, rate_gain, 0.0
    )
    return (
        layer_out,
        grad_tokens,
        qkv_new,
        out_new,
        lift_new,
        down_new,
        gains_new,
        qkv_moment,
        out_moment,
        lift_moment,
        down_moment,
        gains_moment,
        qkv_variance,
        out_variance,
        lift_variance,
        down_variance,
        gains_variance,
        grad_norm,
    )


def solution(mesh):
    placed = (
        P("dp", None),
        P("dp", None),
        P("dp", None),
        P(None, "dp", "tensor"),
        P(("tensor", "dp"), None),
        P(None, "dp", "tensor"),
        P(("tensor", "dp"), None),
        P(None, "dp"),
        P(None, "dp", "tensor"),
        P(("tensor", "dp"), None),
        P(None, "dp", "tensor"),
        P(("tensor", "dp"), None),
        P(None, "dp"),
        P(None, "dp", "tensor"),
        P(("tensor", "dp"), None),
        P(None, "dp", "tensor"),
        P(("tensor", "dp"), None),
        P(None, "dp"),
    )
    def layer(*arrays):
        heads = 4 * arrays[3].shape[2] // HD
        wide = lax.axis_size("tensor") == 4 and 2 * lax.axis_size("dp") == heads
        return (on_device_wide if wide else on_device)(*arrays)

    return jax.shard_map(
        layer,
        mesh=mesh,
        in_specs=placed,
        out_specs=(
            P("dp", None),
            P("dp", None),
            P(None, "dp", "tensor"),
            P(("tensor", "dp"), None),
            P(None, "dp", "tensor"),
            P(("tensor", "dp"), None),
            P(None, "dp"),
            P(None, "dp", "tensor"),
            P(("tensor", "dp"), None),
            P(None, "dp", "tensor"),
            P(("tensor", "dp"), None),
            P(None, "dp"),
            P(None, "dp", "tensor"),
            P(("tensor", "dp"), None),
            P(None, "dp", "tensor"),
            P(("tensor", "dp"), None),
            P(None, "dp"),
            P(),
        ),
        check_vma=False,
    )
```

```python
import math

import jax
import jax.numpy as jnp
from jax import lax
from jax.experimental import pallas as pl
from jax.sharding import PartitionSpec as P


HD = 128
STEP = 10
CLIP_NORM = 16384


norm_eps = 1e-05
beta_one = 0.9
beta_two = 0.95
adam_eps = 1e-08
rate_matrix = 0.02
rate_gain = 0.5
decay_matrix = 0.1


def norm_forward(rows, gain):
    inverse = lax.rsqrt(jnp.mean(rows * rows, axis=-1, keepdims=True) + norm_eps)
    scaled = rows * inverse
    return (scaled, inverse, (scaled * gain).astype(jnp.bfloat16))


def norm_backward(incoming, scaled, inverse, gain):
    grad_gain = jnp.sum(incoming * scaled, axis=0)
    weighted = incoming * gain
    grad_rows = inverse * (weighted - scaled * jnp.mean(weighted * scaled, axis=-1, keepdims=True))
    return (grad_gain, grad_rows)


def block_probs(queries, keys, doc_row, start, block, scale, offset):
    length = keys.shape[0]
    query_pos = start + jnp.arange(block, dtype=jnp.int32)
    key_pos = jnp.arange(length, dtype=jnp.int32)
    allowed = (query_pos[:, None] >= key_pos[None, :]) & (doc_row[:, None] == doc_row[None, :])
    scores = (
        jnp.einsum("qhd,khd->hqk", queries, keys, preferred_element_type=jnp.float32) * scale
        + offset
    )
    probs = jnp.where(allowed[None], jax.nn.sigmoid(scores), 0.0)
    return (queries, probs)


def adam_step(weight, first, second, grad, factor, rate, decay):
    clipped = grad * factor
    moment = beta_one * first + (1.0 - beta_one) * clipped
    variance = beta_two * second + (1.0 - beta_two) * clipped * clipped
    corr_one = 1.0 - beta_one**STEP
    corr_two = 1.0 - beta_two**STEP
    update = moment / corr_one / (jnp.sqrt(variance / corr_two) + adam_eps)
    return (weight - rate * (update + decay * weight), moment, variance)


def on_device(
    tokens,
    documents,
    cotangent,
    qkv_weight,
    out_weight,
    lift_weight,
    down_weight,
    gains,
    qkv_first,
    out_first,
    lift_first,
    down_first,
    gains_first,
    qkv_second,
    out_second,
    lift_second,
    down_second,
    gains_second,
):
    bf16 = jnp.bfloat16
    f32 = jnp.float32
    w_qkv, w_out, w_lift, w_down, w_gains = (
        lax.all_gather(qkv_weight.astype(bf16), "dp", axis=1, tiled=True),
        lax.all_gather(out_weight.astype(bf16), "dp", axis=0, tiled=True),
        lax.all_gather(lift_weight.astype(bf16), "dp", axis=1, tiled=True),
        lax.all_gather(down_weight.astype(bf16), "dp", axis=0, tiled=True),
        lax.all_gather(gains.astype(bf16), "dp", axis=1, tiled=True),
    )
    length = tokens.shape[0]
    local_width = w_qkv.shape[2]
    heads = local_width // HD
    block = min(512, length)
    blocks = length // block
    scale = 1.0 / math.sqrt(HD)
    offset = -math.log(length)
    doc_row = documents[0]
    gain_one = w_gains[0].astype(f32)
    gain_two = w_gains[1].astype(f32)
    x_rows = tokens.astype(f32)
    scaled_one, inverse_one, normed_one = norm_forward(x_rows, gain_one)
    project = jnp.einsum("td,cde->cte", normed_one, w_qkv, preferred_element_type=f32).astype(bf16)
    queries = project[0].reshape(length, heads, HD)
    keys = project[1].reshape(length, heads, HD)
    values = project[2].reshape(length, heads, HD)

    def attend(index):
        start = index * block
        _, probs = block_probs(queries, keys, doc_row, start, block, scale, offset)
        return jnp.einsum(
            "hqk,khd->qhd", probs.astype(bf16), values, preferred_element_type=f32
        ).astype(bf16)

    attended = lax.map(attend, jnp.arange(blocks, dtype=jnp.int32)).reshape(length, local_width)
    branch = lax.psum(jnp.dot(attended, w_out, preferred_element_type=f32), "tensor")
    middle = x_rows + branch
    scaled_two, inverse_two, normed_two = norm_forward(middle, gain_two)
    gate_up = jnp.einsum("td,cde->cte", normed_two, w_lift, preferred_element_type=f32)
    gate = gate_up[0]
    upward = gate_up[1]
    sigma = jax.nn.sigmoid(gate)
    hidden = (gate * sigma * upward).astype(bf16)
    feed = lax.psum(
        jnp.dot(hidden, w_down, preferred_element_type=f32).astype(jnp.bfloat16), "tensor"
    ).astype(jnp.float32)
    layer_out = (middle + feed).astype(bf16)
    grad_incoming = cotangent.astype(f32)
    grad_down = jnp.einsum("tf,td->fd", hidden, cotangent, preferred_element_type=f32)
    grad_hidden = jnp.einsum("td,fd->tf", cotangent, w_down, preferred_element_type=f32)
    grad_gate = (grad_hidden * upward * sigma * (1.0 + gate * (1.0 - sigma))).astype(bf16)
    grad_up = (grad_hidden * gate * sigma).astype(bf16)
    grad_pair = jnp.stack([grad_gate, grad_up])
    grad_lift = jnp.einsum("td,ctf->cdf", normed_two, grad_pair, preferred_element_type=f32)
    back_two = lax.psum(
        jnp.einsum("ctf,cdf->td", grad_pair, w_lift, preferred_element_type=f32), "tensor"
    )
    grad_gain_two, grad_mid_norm = norm_backward(back_two, scaled_two, inverse_two, gain_two)
    grad_mid = grad_incoming + grad_mid_norm
    grad_branch = grad_mid.astype(bf16)
    grad_out = jnp.einsum("te,td->ed", attended, grad_branch, preferred_element_type=f32)
    grad_attended = jnp.einsum("td,ed->te", grad_branch, w_out, preferred_element_type=f32).astype(
        bf16
    )
    grad_heads = grad_attended.reshape(length, heads, HD)

    def attend_back(carry, index):
        grad_keys, grad_values = carry
        start = index * block
        query_block, probs = block_probs(queries, keys, doc_row, start, block, scale, offset)
        grad_probs = jnp.einsum("qhd,khd->hqk", grad_heads, values, preferred_element_type=f32)
        grad_scores = (grad_probs * probs * (1.0 - probs)).astype(bf16)
        grad_query = (
            jnp.einsum("hqk,khd->qhd", grad_scores, keys, preferred_element_type=f32) * scale
        )
        grad_keys = (
            grad_keys
            + jnp.einsum("hqk,qhd->khd", grad_scores, query_block, preferred_element_type=f32)
            * scale
        )
        grad_values = grad_values + jnp.einsum(
            "hqk,qhd->khd", probs.astype(bf16), grad_heads, preferred_element_type=f32
        )
        return ((grad_keys, grad_values), grad_query)

    zeros_kv = jnp.zeros((length, heads, HD), f32)
    (grad_keys, grad_values), grad_queries = lax.scan(
        attend_back, (zeros_kv, zeros_kv), jnp.arange(blocks, dtype=jnp.int32)
    )
    grad_project = jnp.stack(
        [
            grad_queries.reshape(length, local_width),
            grad_keys.reshape(length, local_width),
            grad_values.reshape(length, local_width),
        ]
    ).astype(bf16)
    grad_qkv = jnp.einsum("td,cte->cde", normed_one, grad_project, preferred_element_type=f32)
    back_one = lax.psum(
        jnp.einsum("cte,cde->td", grad_project, w_qkv, preferred_element_type=f32), "tensor"
    )
    grad_gain_one, grad_x_norm = norm_backward(back_one, scaled_one, inverse_one, gain_one)
    grad_tokens = grad_mid + grad_x_norm
    grad_gains = jnp.stack([grad_gain_one, grad_gain_two])
    red_qkv, red_out, red_lift, red_down, red_gains = (
        lax.psum_scatter(grad_qkv, "dp", scatter_dimension=1, tiled=True),
        lax.psum_scatter(grad_out, "dp", scatter_dimension=0, tiled=True),
        lax.psum_scatter(grad_lift, "dp", scatter_dimension=1, tiled=True),
        lax.psum_scatter(grad_down, "dp", scatter_dimension=0, tiled=True),
        lax.psum_scatter(grad_gains, "dp", scatter_dimension=1, tiled=True),
    )
    local_total = (
        jnp.sum(red_qkv * red_qkv)
        + jnp.sum(red_out * red_out)
        + jnp.sum(red_lift * red_lift)
        + jnp.sum(red_down * red_down)
        + jnp.sum(red_gains * red_gains) / lax.axis_size("tensor")
    )
    total = lax.psum(local_total, ("dp", "tensor"))
    grad_norm = jnp.sqrt(total)
    factor = CLIP_NORM / jnp.maximum(grad_norm, CLIP_NORM)
    qkv_new, qkv_moment, qkv_variance = adam_step(
        qkv_weight, qkv_first, qkv_second, red_qkv, factor, rate_matrix, decay_matrix
    )
    out_new, out_moment, out_variance = adam_step(
        out_weight, out_first, out_second, red_out, factor, rate_matrix, decay_matrix
    )
    lift_new, lift_moment, lift_variance = adam_step(
        lift_weight, lift_first, lift_second, red_lift, factor, rate_matrix, decay_matrix
    )
    down_new, down_moment, down_variance = adam_step(
        down_weight, down_first, down_second, red_down, factor, rate_matrix, decay_matrix
    )
    gains_new, gains_moment, gains_variance = adam_step(
        gains, gains_first, gains_second, red_gains, factor, rate_gain, 0.0
    )
    return (
        layer_out,
        grad_tokens,
        qkv_new,
        out_new,
        lift_new,
        down_new,
        gains_new,
        qkv_moment,
        out_moment,
        lift_moment,
        down_moment,
        gains_moment,
        qkv_variance,
        out_variance,
        lift_variance,
        down_variance,
        gains_variance,
        grad_norm,
    )


def after(v, *earlier):
    return lax.optimization_barrier((v, earlier))[0] if earlier else v


def across(v):
    return lax.all_to_all(v, "dp", 0, 0, tiled=True)


def swap_tensor(v, mask):
    return lax.ppermute(v, "tensor", [(i, i ^ mask) for i in range(lax.axis_size("tensor"))])


def swap_dp(v, mask):
    return lax.ppermute(v, "dp", [(i, i ^ mask) for i in range(lax.axis_size("dp"))])


def shift_z(v, step):
    size = lax.axis_size("dp")
    return lax.ppermute(v, "dp", [(i, (i + 2 * step) % size) for i in range(size)])


def in_order(pieces, part, axis):
    even = part % 2 == 0
    low = part < 2
    near = (jnp.where(even, pieces[0], pieces[1]), jnp.where(even, pieces[1], pieces[0]))
    far = (jnp.where(even, pieces[2], pieces[3]), jnp.where(even, pieces[3], pieces[2]))
    first = [jnp.where(low, a, b) for a, b in zip(near, far)]
    last = [jnp.where(low, b, a) for a, b in zip(near, far)]
    return jnp.concatenate(first + last, axis)


def exchange(pieces, part, axis):
    moved = [pieces(part)] + [swap_tensor(pieces(part ^ mask), mask) for mask in (1, 2, 3)]
    return in_order(moved, part, axis)


def four(mine, *earlier):
    far = swap_tensor(after(mine, *earlier), 2)
    return [mine, swap_tensor(mine, 1), far, swap_tensor(far, 1)]


def join_four(mine, part, axis, *earlier):
    return in_order(four(mine, *earlier), part, axis)


def reduce_far(piece_of):
    far = swap_tensor(piece_of(3).astype(jnp.bfloat16), 1).astype(jnp.float32) + piece_of(2)
    return far.astype(jnp.bfloat16)


def reduce_four(far, piece_of):
    near = swap_tensor(piece_of(1).astype(jnp.bfloat16), 1).astype(jnp.float32) + piece_of(0)
    return near + far.astype(jnp.float32)


def gather_rows(own, before_y=(), before_last=()):
    ring = lax.axis_size("dp") // 2
    moved = {}
    for step in (1, ring - 1, *range(2, ring - 1)):
        moved[step] = shift_z(own, step)
    column = [own] + [moved[step] for step in range(1, ring)]
    other = []
    for step, piece in enumerate(column):
        gates = before_y + (before_last if step == ring - 1 else ())
        other.append(swap_dp(after(piece, *gates), 1))
    return jnp.concatenate(column + other, 0), moved[2]


def scatter_y(partial, rows, before_last=()):
    ring = lax.axis_size("dp") // 2
    slots = partial.reshape(2, ring, rows, partial.shape[-1])
    here = {}
    for step in (*range(ring - 2, 0, -1), ring - 1, 0):
        sent = slots[1, step].astype(jnp.bfloat16)
        if step == 0:
            sent = after(sent, *before_last)
        here[step] = slots[0, step] + swap_dp(sent, 1).astype(jnp.float32)
    return here


def scatter_z(here, before=(), before_sum=()):
    ring = lax.axis_size("dp") // 2
    total = here[0]
    for step in (*range(ring - 2, 0, -1), ring - 1):
        moved = shift_z(after(here[step].astype(jnp.bfloat16), *before), -step)
        total = total + after(moved, *before_sum).astype(jnp.float32)
    return total


def dot(a, b):
    return jnp.dot(a, b, preferred_element_type=jnp.float32)


def dot_t(a, b):
    return lax.dot_general(a, b, (((1,), (1,)), ((), ())), preferred_element_type=jnp.float32)


def t_dot(a, b):
    return lax.dot_general(a, b, (((0,), (0,)), ((), ())), preferred_element_type=jnp.float32)


def head_probs(row_docs, column_docs, project, head):
    length = project.shape[1]
    heads = project.shape[2] // (3 * HD)
    queries, keys, values = (
        project[0, :, (c * heads + head) * HD : (c * heads + head + 1) * HD] for c in range(3)
    )
    scores = dot_t(queries, keys) * (1.0 / math.sqrt(HD)) - math.log(length)
    query = lax.broadcasted_iota(jnp.int32, scores.shape, 0)
    key = lax.broadcasted_iota(jnp.int32, scores.shape, 1)
    allowed = (query >= key) & (column_docs[0] == row_docs[0])
    return queries, keys, values, jnp.where(allowed, jax.nn.sigmoid(scores), 0.0)


def attend_kernel(row_docs, column_docs, project, out):
    for head in range(project.shape[2] // (3 * HD)):
        unused, unused, values, probs = head_probs(row_docs, column_docs, project, head)
        attended = dot(probs.astype(jnp.bfloat16), values)
        out[0, :, head * HD : (head + 1) * HD] = attended.astype(jnp.bfloat16)


def attend_back_kernel(row_docs, column_docs, project, grad, out):
    bf16 = jnp.bfloat16
    scale = 1.0 / math.sqrt(HD)
    heads = project.shape[2] // (3 * HD)
    for head in range(heads):
        queries, keys, values, probs = head_probs(row_docs, column_docs, project, head)
        grad_head = grad[0, :, head * HD : (head + 1) * HD]
        grad_scores = (dot_t(grad_head, values) * probs * (1.0 - probs)).astype(bf16)
        grads = (
            dot(grad_scores, keys) * scale,
            t_dot(grad_scores, queries) * scale,
            t_dot(probs.astype(bf16), grad_head),
        )
        for c in range(3):
            at = (c * heads + head) * HD
            out[0, :, at : at + HD] = grads[c].astype(bf16)


def attend_call(kernel, docs, project, others, features):
    arrays = [docs[:, None], docs[:, :, None], project, *others]
    return pl.pallas_call(
        kernel,
        grid=(project.shape[0],),
        in_specs=[pl.BlockSpec((1,) + v.shape[1:], lambda s: (s, 0, 0)) for v in arrays],
        out_specs=pl.BlockSpec((1, project.shape[1], features), lambda s: (s, 0, 0)),
        out_shape=jax.ShapeDtypeStruct(project.shape[:2] + (features,), jnp.bfloat16),
    )(*arrays)


def on_device_wide(
    tokens,
    documents,
    cotangent,
    qkv_weight,
    out_weight,
    lift_weight,
    down_weight,
    gains,
    qkv_first,
    out_first,
    lift_first,
    down_first,
    gains_first,
    qkv_second,
    out_second,
    lift_second,
    down_second,
    gains_second,
):
    bf16 = jnp.bfloat16
    f32 = jnp.float32
    size = lax.axis_size("dp")
    ring = size // 2
    place = lax.axis_index("dp")
    part = lax.axis_index("tensor")
    length, width = tokens.shape
    rows = length // 4
    block = qkv_weight.shape[1]
    quarter = block // 4
    units = lift_weight.shape[2] // size
    pair = 2 * HD

    def own_rows(v):
        return lax.dynamic_slice_in_dim(v, part * rows, rows, 0)

    def take(v, index, axis):
        return lax.dynamic_index_in_dim(v, index, axis, keepdims=True)

    own_tokens = own_rows(tokens)
    own_cot = own_rows(cotangent)
    x_rows = own_tokens.astype(f32)

    qkv_low = qkv_weight.astype(bf16).reshape(3, 4, quarter, qkv_weight.shape[2])
    plane = exchange(lambda k: take(qkv_low, k, 1)[:, 0], part, 2)
    w_head = [
        jnp.concatenate([plane[c, :, k * pair : (k + 1) * pair] for c in range(3)], 1)
        for k in range(size)
    ]
    head_mine = across(jnp.stack(w_head))
    w_head = join_four(head_mine[:, None], part, 1).reshape(width, 3 * pair)

    small = jnp.concatenate([gains.astype(bf16), documents.astype(bf16)], 0)
    small = jnp.pad(small.reshape(1, -1), ((0, 7), (0, width - small.size)))
    all_tokens, unused = gather_rows(jnp.concatenate([own_tokens, small], 0), (), (head_mine,))
    all_tokens = all_tokens.reshape(size, rows + 8, width)
    small = all_tokens[:, rows, : 3 * gains.shape[1]]
    all_tokens = all_tokens[:, :rows].reshape(size * rows, width)
    slot = jnp.arange(size, dtype=jnp.int32)
    slot = (place % 2 ^ slot % 2) * ring + (place // 2 - slot // 2) % ring
    owner = (slot[:, None] == jnp.arange(size, dtype=jnp.int32)[None]).astype(bf16)
    w_gains = dot(owner, small[:, : 2 * gains.shape[1]])
    w_gains = w_gains.reshape(size, 2, gains.shape[1]).transpose(1, 0, 2).reshape(2, width)
    gain_one = w_gains[0]
    gain_two = w_gains[1]
    docs = lax.dynamic_slice_in_dim(small[:, 2 * gains.shape[1] :], 2 * part, 2, 0).astype(f32)

    to_head = [
        (4 * d + t, 4 * (2 * t + d // 4) + d % 4) for d in range(size) for t in range(4)
    ]
    w_rows = lax.ppermute(after(out_weight, plane).astype(bf16), ("dp", "tensor"), to_head)
    w_rows = join_four(w_rows, part, 0)


    w_lift = lift_weight.astype(bf16)
    w_lift = jnp.concatenate(
        [w_lift[c, :, k * units : (k + 1) * units][None] for k in range(size) for c in range(2)],
        0,
    )
    w_lift = w_lift.reshape(size, 2 * block, units)
    lift_mine = across(after(w_lift, head_mine))

    def to_sequences(v):
        v = v.reshape(4, 2, 1, rows, v.shape[-1])
        v = exchange(lambda k: take(v, k, 0)[0], part, 1)
        return v.reshape(2, length, v.shape[-1])

    def to_quarters(v):
        v = v.reshape(2, 4, rows, v.shape[-1])
        v = exchange(lambda k: take(v, k, 1)[None, :, 0], part, 0)
        return v.reshape(size * rows, v.shape[-1])

    normed_one = norm_forward(all_tokens.astype(f32), gain_one)[2]
    project = dot(normed_one, w_head).astype(bf16)
    own_cot_late = after(own_cot, project)
    project = to_sequences(project)
    attended = attend_call(attend_kernel, docs, project, [], pair)
    attended = to_quarters(attended)

    w_lift = [v.reshape(size, 2, block, units) for v in four(lift_mine, attended)]
    w_lift = [v[:, c].reshape(width, units) for c in range(2) for v in w_lift]
    w_lift = jnp.concatenate(w_lift, 1)
    w_down = jnp.concatenate(four(down_weight.astype(bf16), attended), 0)

    branch = scatter_y(dot(attended, w_rows), rows)
    all_cot, unused = gather_rows(own_cot_late, ())
    branch = after(scatter_z(branch), all_cot)
    middle = x_rows + branch
    scaled_two, inverse_two, normed_two = norm_forward(middle, gain_two)
    normed_two, unused = gather_rows(normed_two)

    gate_up = dot(normed_two, w_lift)
    gate = gate_up[:, : 4 * units]
    upward = gate_up[:, 4 * units :]
    sigma = jax.nn.sigmoid(gate)
    hidden = (gate * sigma * upward).astype(bf16)
    grad_hidden = dot_t(all_cot, w_down)
    grad_gate = (grad_hidden * upward * sigma * (1.0 + gate * (1.0 - sigma))).astype(bf16)
    grad_up = (grad_hidden * gate * sigma).astype(bf16)
    grad_pair = jnp.concatenate([grad_gate, grad_up], 1)

    def unit_block(v, delta):
        return v[:, delta * units : (delta + 1) * units]

    def down_piece(delta):
        return t_dot(unit_block(hidden, delta), all_cot)

    def lift_piece(delta):
        own = [unit_block(grad_gate, delta), unit_block(grad_up, delta)]
        return t_dot(normed_two, jnp.concatenate(own, 1))

    lift_far = reduce_far(lift_piece)
    down_far = reduce_far(down_piece)
    back_two = scatter_y(dot_t(grad_pair, w_lift), rows, (lift_far, down_far))
    feed = scatter_y(dot(after(hidden, back_two[2]), w_down), rows)
    back_two = scatter_z(back_two)
    grad_gain_two, grad_mid_norm = norm_backward(back_two, scaled_two, inverse_two, gain_two)
    grad_mid = own_cot.astype(f32) + grad_mid_norm
    all_branch, mid_moved = gather_rows(grad_mid.astype(bf16))
    lift_moved = swap_tensor(lift_far, 2)
    lift_sum = reduce_four(lift_moved, lift_piece).astype(bf16)
    lift_home = across(lift_sum.reshape(size, block, 2 * units))
    red_lift = [
        jnp.concatenate([lift_home[k, :, c * units : (c + 1) * units] for k in range(size)], 1)
        for c in range(2)
    ]
    red_lift = lax.optimization_barrier(jnp.stack(red_lift)).astype(f32)

    all_branch = after(all_branch, lift_sum)
    grad_heads = to_sequences(dot_t(all_branch, w_rows).astype(bf16))
    grad_project = attend_call(attend_back_kernel, docs, project, [grad_heads], 3 * pair)
    grad_project = to_quarters(grad_project)

    down_moved = swap_tensor(after(down_far, grad_project), 2)
    grad_head = t_dot(after(normed_one, middle), grad_project).reshape(size, 4, quarter, 3 * pair)

    def head_piece(delta):
        return take(grad_head, part ^ delta, 1)[:, 0]

    head_moved = reduce_far(head_piece)
    head_moved = swap_tensor(head_moved, 2)
    grad_head_sum = reduce_four(head_moved, head_piece).astype(bf16)
    by_head = across(after(grad_head_sum, lift_home))
    red_down = reduce_four(after(down_moved, by_head), down_piece)
    back_one = dot_t(grad_project, w_head)
    back_one = scatter_z(scatter_y(back_one, rows))

    def head_pair(k):
        both = lax.dynamic_slice_in_dim(by_head, 2 * k, 2, 0)
        return jnp.stack(
            [
                jnp.concatenate([both[j, :, c * pair : (c + 1) * pair] for j in range(2)], 1)
                for c in range(3)
            ]
        )

    red_qkv = exchange(head_pair, part, 1)
    red_qkv = lax.optimization_barrier(red_qkv).astype(f32)

    grad_out = t_dot(attended, after(all_branch, grad_project)).reshape(4, pair // 4, width)

    def out_piece(delta):
        return take(grad_out, part ^ delta, 0)[0]

    out_moved = swap_tensor(reduce_far(out_piece), 2)
    red_out = reduce_four(out_moved, out_piece).astype(bf16)
    red_out = lax.ppermute(red_out, ("dp", "tensor"), [(b, a) for a, b in to_head])
    red_out = red_out.astype(f32)

    scaled_one, inverse_one, unused = norm_forward(x_rows, gain_one)
    grad_gain_one, grad_x_norm = norm_backward(back_one, scaled_one, inverse_one, gain_one)
    own_grad = grad_mid + grad_x_norm
    feed = scatter_z(feed, (mid_moved,), (back_one,))
    own_out = (middle + feed).astype(bf16)

    local_total = (
        jnp.sum(red_qkv * red_qkv)
        + jnp.sum(red_out * red_out)
        + jnp.sum(red_lift * red_lift)
        + jnp.sum(red_down * red_down)
    )
    totals = jnp.concatenate(
        [
            jnp.stack([grad_gain_one, grad_gain_two]).reshape(-1, 128),
            jnp.broadcast_to(local_total, (8, 128)),
        ]
    )
    for mask in (1, 2):
        totals = totals + swap_tensor(totals, mask)
    halfway = totals
    mask = 1
    while mask < size:
        totals = totals + swap_dp(totals, mask)
        mask *= 2
    layer_out = join_four(own_out, part, 0, halfway)
    grad_tokens = join_four(own_grad, part, 0, halfway)
    grad_gains = totals[:-8].reshape(2, width)
    grad_norm = jnp.sqrt(totals[-1, 0] + jnp.sum(grad_gains * grad_gains))
    red_gains = lax.dynamic_slice_in_dim(grad_gains, place * gains.shape[1], gains.shape[1], 1)
    factor = CLIP_NORM / jnp.maximum(grad_norm, CLIP_NORM)
    qkv_new, qkv_moment, qkv_variance = adam_step(
        qkv_weight, qkv_first, qkv_second, red_qkv, factor, rate_matrix, decay_matrix
    )
    out_new, out_moment, out_variance = adam_step(
        out_weight, out_first, out_second, red_out, factor, rate_matrix, decay_matrix
    )
    lift_new, lift_moment, lift_variance = adam_step(
        lift_weight, lift_first, lift_second, red_lift, factor, rate_matrix, decay_matrix
    )
    down_new, down_moment, down_variance = adam_step(
        down_weight, down_first, down_second, red_down, factor, rate_matrix, decay_matrix
    )
    gains_new, gains_moment, gains_variance = adam_step(
        gains, gains_first, gains_second, red_gains, factor, rate_gain, 0.0
    )
    return (
        layer_out,
        grad_tokens,
        qkv_new,
        out_new,
        lift_new,
        down_new,
        gains_new,
        qkv_moment,
        out_moment,
        lift_moment,
        down_moment,
        gains_moment,
        qkv_variance,
        out_variance,
        lift_variance,
        down_variance,
        gains_variance,
        grad_norm,
    )


def solution(mesh):
    placed = (
        P("dp", None),
        P("dp", None),
        P("dp", None),
        P(None, "dp", "tensor"),
        P(("tensor", "dp"), None),
        P(None, "dp", "tensor"),
        P(("tensor", "dp"), None),
        P(None, "dp"),
        P(None, "dp", "tensor"),
        P(("tensor", "dp"), None),
        P(None, "dp", "tensor"),
        P(("tensor", "dp"), None),
        P(None, "dp"),
        P(None, "dp", "tensor"),
        P(("tensor", "dp"), None),
        P(None, "dp", "tensor"),
        P(("tensor", "dp"), None),
        P(None, "dp"),
    )

    def layer(*arrays):
        heads = 4 * arrays[3].shape[2] // HD
        wide = lax.axis_size("tensor") == 4 and 2 * lax.axis_size("dp") == heads
        if not wide:
            return on_device(*arrays)
        return on_device_wide(*arrays)

    return jax.shard_map(
        layer,
        mesh=mesh,
        in_specs=placed,
        out_specs=(
            P("dp", None),
            P("dp", None),
            P(None, "dp", "tensor"),
            P(("tensor", "dp"), None),
            P(None, "dp", "tensor"),
            P(("tensor", "dp"), None),
            P(None, "dp"),
            P(None, "dp", "tensor"),
            P(("tensor", "dp"), None),
            P(None, "dp", "tensor"),
            P(("tensor", "dp"), None),
            P(None, "dp"),
            P(None, "dp", "tensor"),
            P(("tensor", "dp"), None),
            P(None, "dp", "tensor"),
            P(("tensor", "dp"), None),
            P(None, "dp"),
            P(),
        ),
        check_vma=False,
    )
```
